256 devices in a mesh: row: 16 (over y, x), col: 16 (over z, core).
Axes of the slice: x: 4, y: 4, z: 8, core: 2. Of those that a mesh axis runs over, the one named last changes fastest.
Arguments:
- source: float32 [2048, 64, 128], P(('row', 'col')), may hold values from -6 to 6
- blocks: float32 [65536, 64, 64], P(('row', 'col')), may hold values from -0.15625 to 0.15625
- row_index: int32 [65536], P(('row', 'col')), may hold values from 0 to 127
- col_index: int32 [65536], P(('row', 'col')), may hold values from 0 to 127
- live_count: int32 [256], P(('row', 'col')), may hold values from 64 to 256, as said below
Outputs:
- irradiance: float32 [2048, 64, 128], P(('row', 'col'))
The draws below stay inside these ranges and needn't reach their ends.
Inputs may be any that keep to these rules, and one draw needn't show every extreme that they name: `live_count`: slots of a device beyond its live count are padding; some device has all 256 slots live.
All inputs are finite; a program needn't handle non-finite values.
Results may differ from the reference program's by a relative error of at most 0.0003.
Values sent between devices are 32-bit elements; how exact they have to be, the bound alone decides.
A program may use at most 128 MiB of HBM per device.

```python
import jax
import jax.numpy as jnp
from jax import lax

BLOCK = 64
LIGHTS = 128
SLOTS = 32
ITERS = 2
BR_DEV = 8
NNZ_DEV = 256
BRICKS = 2048
N_ROW = 16
N_COL = 16


def draw_live_count(key, part):
    counts = jax.random.randint(key, (N_ROW * N_COL,), NNZ_DEV // 4, NNZ_DEV + 1)
    chosen = jax.random.randint(jax.random.fold_in(key, 7), (), 0, N_ROW * N_COL)
    return counts.at[chosen].set(NNZ_DEV).astype(jnp.int32)


def place_ends(array, rng, smallest, largest):
    longest = array.shape.index(max(array.shape))
    spots = []
    for shift in (0, 1):
        where = [jax.random.randint(jax.random.fold_in(rng, axis), (), 0, length) for axis, length in enumerate(array.shape)]
        where[longest] = (where[longest] + shift) % array.shape[longest]
        spots.append(tuple(where))
    return array.at[spots[0]].set(smallest).at[spots[1]].set(largest)


def levels(key, shape, shards, low, high):
    def one(axis_at, blocks):
        draws = jax.random.uniform(jax.random.fold_in(jax.random.fold_in(key, 6), axis_at), (blocks,), jnp.float32, low / len(shards), high / len(shards))
        return jnp.repeat(jnp.exp(draws), shape[axis_at] // blocks).reshape((-1,) + (1,) * (len(shape) - axis_at - 1))

    factor_of = one(*shards[0])
    for cut in shards[1:]:
        factor_of = factor_of * one(*cut)
    return factor_of


def normal_values(key, extent, deviation, limit, split=(), kind=jnp.bfloat16):
    values = deviation * jax.random.normal(key, extent, jnp.float32)
    if split:
        values = values * levels(key, extent, split, -0.22, 0.18)
    return jnp.clip(values, -limit, limit).astype(kind)


def setup_inputs(seed: int = 0) -> dict:
    streams_of = jax.random.split(jax.random.key(seed), 6)
    return {
        "source": normal_values(streams_of[0], (BRICKS, BLOCK, LIGHTS), 1.0, 6.0, ((0, 256),), jnp.float32),
        "blocks": normal_values(streams_of[1], (BRICKS * SLOTS, BLOCK, BLOCK), (BLOCK * 20) ** -0.5, 0.15625, ((0, 256),), jnp.float32),
        "row_index": place_ends(jax.random.randint(streams_of[2], (BRICKS * SLOTS,), 0, BR_DEV * N_COL), jax.random.fold_in(streams_of[2], 1), 0, (BR_DEV * N_COL) - 1).astype(jnp.int32),
        "col_index": place_ends(jax.random.randint(streams_of[3], (BRICKS * SLOTS,), 0, BR_DEV * N_ROW), jax.random.fold_in(streams_of[3], 1), 0, (BR_DEV * N_ROW) - 1).astype(jnp.int32),
        "live_count": draw_live_count(jax.random.fold_in(streams_of[5], 71), 0),
    }


def transfer(field, blocks, row_index, col_index, live_count):
    group_rows = BR_DEV * N_COL
    slot_ids = jnp.arange(NNZ_DEV, dtype=jnp.int32)

    def row_group(r):
        def over_col(running, c):
            device = (r * N_COL + c).astype(jnp.int32)
            first = (device * NNZ_DEV).astype(jnp.int32)
            block_set = lax.dynamic_slice_in_dim(blocks, first, NNZ_DEV, 0)
            rows_here = lax.dynamic_slice_in_dim(row_index, first, NNZ_DEV, 0)
            cols_here = lax.dynamic_slice_in_dim(col_index, first, NNZ_DEV, 0)
            live_mask = slot_ids < live_count[device]
            global_col = (((cols_here // BR_DEV) * N_COL + c) * BR_DEV + cols_here % BR_DEV).astype(jnp.int32)
            picked = jnp.take(field, global_col, axis=0)
            products = jnp.einsum("nij,njl->nil", block_set, picked, precision=lax.Precision.HIGHEST)
            products = jnp.where(live_mask[:, None, None], products, jnp.zeros_like(products))
            return running + jax.ops.segment_sum(products, rows_here, num_segments=group_rows), None

        start = jnp.zeros((group_rows, field.shape[1], field.shape[2]), jnp.float32)
        result, _ = lax.scan(over_col, start, jnp.arange(N_COL, dtype=jnp.int32))
        return result

    stacked = lax.map(row_group, jnp.arange(N_ROW, dtype=jnp.int32))
    return stacked.reshape(field.shape)


def reference(source, blocks, row_index, col_index, live_count):
    field = source
    for bounce in range(ITERS):
        field = source + transfer(field, blocks, row_index, col_index, live_count)
    return field
```

```python
import jax
import jax.numpy as jnp
from jax import lax
from jax.experimental import pallas as pl
from jax.experimental.pallas import tpu as pltpu
from jax.sharding import PartitionSpec as P

MESH = pl.DeviceIdType.MESH
ITERS = 2
GROUPS = 2
TILES = 4
SLOTS = 256
ROWS = 16
ZN = 8
ZSHIFT = (4, 3, 5, 2, 6, 1, 7, 0)
UNROLL = 8
PIECES = 8
LINES = (0, 3, 1, 2)
OFF = (0, 2, 6, 10)
SPAN = 14


def rem(a, n):
    return lax.rem(a, n)


class Schedule:
    def __init__(self):
        self.tasks = []

    def add(self, when, run):
        self.tasks.append((when, len(self.tasks), run))

    def run(self):
        for _, _, run in sorted(self.tasks, key=lambda task: task[:2]):
            run()


def kernel(
    src_hbm, blk_hbm, rank_ref, mi, mf, out_ref,
    xg, xs0, xs1, a_ref, wide, c_ref, raw, perm, po, px, cx, rp, sp, fx, srcv,
    ag_s, ag_r, cx_s, cx_r, rs_s, rs_r, blk_sem, src_sem,
):
    xs = (xs0, xs1)
    row, col = lax.axis_index("row"), lax.axis_index("col")
    y, x = row // 4, rem(row, 4)
    z, h = col // 2, rem(col, 2)

    def at(i, j):
        return rem(y + i * h + j * (1 - h), 4) * 4 + rem(x + i * (1 - h) + j * h, 4)

    def zcol(d):
        return rem(z + d, ZN) * 2 + h

    partner = z * 2 + (1 - h)

    blk_copies = [
        pltpu.make_async_copy(blk_hbm.at[pl.ds(16 * n, 16)], raw.at[pl.ds(16 * n, 16)], blk_sem.at[n]) for n in range(4)
    ]
    src_copy = pltpu.make_async_copy(src_hbm, srcv, src_sem)
    src_copy.start()
    for copy in blk_copies:
        copy.start()

    barrier = pltpu.get_barrier_semaphore()
    peers = [(at(1, 0), col), (at(3, 0), col), (at(0, 1), col), (at(0, 3), col)]
    peers += [(row, zcol(1)), (row, zcol(7)), (row, partner)]
    for peer in peers:
        pl.semaphore_signal(barrier, inc=1, device_id=peer, device_id_type=MESH)

    lane = lax.broadcasted_iota(jnp.int32, (64, 128), 1)
    low = lane < 64
    half = jnp.where(lax.broadcasted_iota(jnp.int32, (8, 128), 1) < 64, 1.0, 0.0).astype(jnp.float32)
    flip = 1.0 - 2.0 * half

    src_copy.wait()
    for j in range(TILES):
        even, odd = srcv[2 * j], srcv[2 * j + 1]
        xg[row * 8 + j] = jnp.where(low, even, pltpu.roll(odd, 64, 1))
        xg[row * 8 + TILES + j] = jnp.where(low, pltpu.roll(even, 64, 1), odd)

    pl.semaphore_wait(barrier, len(peers))


    def tile0(b, g, r):
        return b * 128 + r * 8 + g * TILES

    def ag(b, g, k, r, t0, n, dest):
        ref = xg.at[pl.ds(tile0(b, g, r) + t0, n)]
        i = (b * GROUPS + g) * 20 + k
        return pltpu.make_async_remote_copy(
            src_ref=ref, dst_ref=ref, send_sem=ag_s.at[i], recv_sem=ag_r.at[i], device_id=(dest, col), device_id_type=MESH
        )

    pending = []

    def go(copy):
        copy.start()
        pending.append(copy)

    def split(b, g, r, t0=0, n=TILES):
        def one(t, carry):
            tile = xg[tile0(b, g, r) + t0 + t]
            for v, val in enumerate((tile, pltpu.roll(tile, 64, 1))):
                hi = val.astype(jnp.bfloat16)
                lo = (val - hi.astype(jnp.float32)).astype(jnp.bfloat16)
                at_ = (r * TILES + t0 + t) * 2 + v
                xs[g][at_, pl.ds(0, 64), :] = hi
                xs[g][at_, pl.ds(64, 64), :] = lo
            return carry

        lax.fori_loop(0, n, one, 0)

    def gather_own(b, g):
        go(ag(b, g, 0, row, 0, 4, at(1, 0)))
        go(ag(b, g, 1, row, 0, 4, at(3, 0)))
        go(ag(b, g, 4, row, 0, 4, at(0, 1)))
        go(ag(b, g, 5, row, 0, 4, at(0, 3)))

    def line_out(b, g, li):
        r = at(LINES[li], 0)
        go(ag(b, g, 4 + 4 * li, r, 0, 4, at(0, 1)))
        go(ag(b, g, 5 + 4 * li, r, 0, 4, at(0, 3)))

    def first_full(b, g, k):
        r = at(3, 0) if k == 0 else at(1, 0)
        ag(b, g, k, r, 0, 4, row).wait_recv()
        if k == 0:
            go(ag(b, g, 2, r, 0, 2, at(1, 0)))
        else:
            go(ag(b, g, 3, r, 2, 2, at(3, 0)))
        line_out(b, g, 1 + k)
        split(b, g, r)

    def first_far(b, g):
        r = at(2, 0)
        ag(b, g, 2, r, 0, 2, row).wait_recv()
        ag(b, g, 3, r, 2, 2, row).wait_recv()
        line_out(b, g, 3)
        split(b, g, r)

    def line_full(b, g, li, k):
        r = at(LINES[li], 3) if k == 0 else at(LINES[li], 1)
        ag(b, g, 4 + 4 * li + k, r, 0, 4, row).wait_recv()
        if k == 0:
            go(ag(b, g, 6 + 4 * li, r, 0, 2, at(0, 1)))
        else:
            go(ag(b, g, 7 + 4 * li, r, 2, 2, at(0, 3)))
        split(b, g, r)

    def line_far(b, g, li):
        r = at(LINES[li], 2)
        ag(b, g, 6 + 4 * li, r, 0, 2, row).wait_recv()
        ag(b, g, 7 + 4 * li, r, 2, 2, row).wait_recv()
        split(b, g, r)


    perm[...] = jnp.where(lax.broadcasted_iota(jnp.int32, (SLOTS, SLOTS), 0) == rank_ref[...], 1.0, 0.0).astype(jnp.bfloat16)

    def sort_blocks(part, n):
        if part == 0:
            blk_copies[n].wait()

        def one(i, carry):
            val = raw[i]
            hi = val.astype(jnp.bfloat16)
            lo = (val - hi.astype(jnp.float32)).astype(jnp.bfloat16)
            four = jnp.concatenate([hi, hi, lo, lo], axis=0)
            order = perm[pl.ds(128 * part, 128), :]
            res = lax.dot_general(order, four, (((1,), (1,)), ((), ())), preferred_element_type=jnp.float32)
            wide[pl.ds(i, 128, stride=128), :] = res[:, :128]
            wide[pl.ds(64 + i, 128, stride=128), :] = res[:, 128:]
            return carry

        lax.fori_loop(16 * n, 16 * n + 16, one, 0)

    def pack_blocks(part):
        def one(p, carry):
            a_ref[128 * part + p] = wide[pl.ds(pl.multiple_of(p * 128, 128), 128), :].astype(jnp.bfloat16)
            return carry

        lax.fori_loop(0, 128, one, 0)


    def products(g, piece):
        start = piece * (SLOTS // PIECES)

        def body(it, acc):
            base = start + it * UNROLL
            found = [
                jnp.dot(a_ref[base + u], xs[g][mi[base + u]], preferred_element_type=jnp.float32) for u in range(UNROLL)
            ]
            for u in range(UNROLL):
                p = base + u
                mask = half + mf[SLOTS + p] * flip
                both = found[u][:64] + found[u][64:]
                both = (both.reshape(8, 8, 128) * mask[None]).reshape(64, 128)
                acc = acc * mf[p] + both
                c_ref[p] = acc
            return acc

        acc = c_ref[start - 1] if piece else jnp.zeros((64, 128), jnp.float32)
        lax.fori_loop(0, SLOTS // PIECES // UNROLL, body, acc)

    def partial_sum(zc, core, t):
        q = (zc * 2 + core) * TILES + t
        return c_ref[mi[SLOTS + q]] * mf[2 * SLOTS + q]

    def cx_copy(b, g, o):
        i = (b * GROUPS + g) * ZN + o
        return pltpu.make_async_remote_copy(
            src_ref=px.at[pl.ds((g * ZN + o) * TILES, TILES)], dst_ref=cx.at[pl.ds(i * TILES, TILES)],
            send_sem=cx_s.at[i], recv_sem=cx_r.at[i], device_id=(row, partner), device_id_type=MESH,
        )

    def sums(b, g):
        if b:
            for o in range(ZN):
                cx_copy(b - 1, g, o).wait_send()
        for o in range(ZN):
            for t in range(TILES):
                px[(g * ZN + o) * TILES + t] = partial_sum(rem(z + ZSHIFT[o], ZN), 1 - h, t)
            if o:
                cx_copy(b, g, o - 1).start()
        for o in range(ZN):
            for t in range(TILES):
                po[(g * ZN + o) * TILES + t] = partial_sum(rem(z + ZSHIFT[o], ZN), h, t)
            if o == 0:
                cx_copy(b, g, ZN - 1).start()


    def rs_copy(b, g, side, t):
        i = (b * GROUPS + g) * 2 + side
        n = 2 if t == 0 else 4
        at_ = pl.ds(i * SPAN + OFF[t], n)
        return pltpu.make_async_remote_copy(
            src_ref=sp.at[at_], dst_ref=rp.at[at_], send_sem=rs_s.at[i * 4 + t], recv_sem=rs_r.at[i * 4 + t],
            device_id=(row, zcol(1 if side == 0 else 7)), device_id_type=MESH,
        )

    def chip_sum(b, g, o, t):
        return po[(g * ZN + o) * TILES + t] + cx[((b * GROUPS + g) * ZN + o) * TILES + t]

    def reduce_step(b, g, t):
        for o in (0,) if t == 0 else (2 * t - 1, 2 * t):
            cx_copy(b, g, o).wait_recv()
        for side in (0, 1):
            base = ((b * GROUPS + g) * 2 + side) * SPAN
            o = 0 if t == 0 else 2 * t - 1 + side
            if t:
                rs_copy(b, g, side, t - 1).wait_recv()
            if t == 0:
                for n in range(2):
                    sp[base + n] = chip_sum(b, g, 0, 2 * side + n)
            else:
                for n in range(4):
                    val = chip_sum(b, g, o, n)
                    if t > 1:
                        val = val + rp[base + OFF[t - 1] + n]
                    elif n // 2 == side:
                        val = val + rp[base + n - 2 * side]
                    sp[base + OFF[t] + n] = val
            go(rs_copy(b, g, side, t))

    def reduce_last(b, g):
        cx_copy(b, g, ZN - 1).wait_recv()
        for side in (0, 1):
            rs_copy(b, g, side, 3).wait_recv()
        base = (b * GROUPS + g) * 2 * SPAN
        for n in range(TILES):
            val = xg[tile0(0, g, row) + n] + chip_sum(b, g, ZN - 1, n)
            val = val + rp[base + OFF[3] + n] + rp[base + SPAN + OFF[3] + n]
            if b + 1 < ITERS:
                xg[tile0(b + 1, g, row) + n] = val
            else:
                fx[g * TILES + n] = val
        if b + 1 < ITERS:
            gather_own(b + 1, g)
            split(b + 1, g, row)

    plan = Schedule()

    def plan_gather(b, g, t0, own):
        if b == 0:
            plan.add(own, lambda: (gather_own(b, g)))
            plan.add(own, lambda: split(b, g, row))
        plan.add(t0 + 3.0, lambda: first_full(b, g, 0))
        plan.add(t0 + 3.2, lambda: first_full(b, g, 1))
        plan.add(t0 + 3.5, lambda: line_full(b, g, 0, 0))
        plan.add(t0 + 3.7, lambda: line_full(b, g, 0, 1))
        plan.add(t0 + 4.8, lambda: first_far(b, g))
        plan.add(t0 + 5.5, lambda: line_full(b, g, 1, 0))
        plan.add(t0 + 5.7, lambda: line_full(b, g, 1, 1))
        plan.add(t0 + 6.5, lambda: line_full(b, g, 2, 0))
        plan.add(t0 + 6.7, lambda: line_full(b, g, 2, 1))
        plan.add(t0 + 7.0, lambda: line_far(b, g, 0))
        plan.add(t0 + 8.5, lambda: line_full(b, g, 3, 0))
        plan.add(t0 + 8.7, lambda: line_full(b, g, 3, 1))
        plan.add(t0 + 9.0, lambda: line_far(b, g, 1))
        plan.add(t0 + 9.7, lambda: line_far(b, g, 2))
        plan.add(t0 + 10.7, lambda: line_far(b, g, 3))

    def plan_products(b, g, t0, step):
        for piece in range(PIECES):
            plan.add(t0 + piece * step, lambda piece=piece: products(g, piece))
        plan.add(t0 + PIECES * step, lambda: sums(b, g))

    def plan_reduce(b, g, t0):
        for t, when in enumerate((1.0, 3.5, 6.5, 9.5)):
            plan.add(t0 + when, lambda t=t: reduce_step(b, g, t))
        plan.add(t0 + 12.5, lambda: reduce_last(b, g))

    for part in range(2):
        for n in range(4):
            plan.add(2.0 + 4.2 * part + 0.9 * n, lambda part=part, n=n: sort_blocks(part, n))
        plan.add(5.6 + 4.2 * part, lambda part=part: pack_blocks(part))
    plan_gather(0, 0, 0.0, 0.0)
    plan_gather(0, 1, 10.5, 3.3)
    plan_products(0, 0, 11.5, 0.5)
    plan_reduce(0, 0, 16.5)
    plan_products(0, 1, 22.5, 0.5)
    plan_reduce(0, 1, 28.0)
    plan_gather(1, 0, 29.0, 29.0)
    plan_products(1, 0, 41.0, 0.5)
    plan_reduce(1, 0, 46.0)
    plan_gather(1, 1, 41.0, 41.0)
    plan_products(1, 1, 53.0, 0.5)
    plan_reduce(1, 1, 58.0)
    plan.run()

    for j in range(TILES):
        first, second = fx[j], fx[TILES + j]
        out_ref[2 * j] = jnp.where(low, first, pltpu.roll(second, 64, 1))
        out_ref[2 * j + 1] = jnp.where(low, pltpu.roll(first, 64, 1), second)

    for copy in pending:
        copy.wait_send()
    for g in range(GROUPS):
        for o in range(ZN):
            cx_copy(ITERS - 1, g, o).wait_send()


def tables(row_index, col_index, live_count):
    slots = jnp.arange(SLOTS, dtype=jnp.int32)
    rows = jnp.where(slots < live_count[0], row_index, 128)
    key = rows * SLOTS + slots
    rank = jnp.sum((key[None, :] < key[:, None]).astype(jnp.int32), axis=1)
    packed = rows * 128 + col_index
    ordered = jnp.sum(jnp.where(rank[None, :] == slots[:, None], packed[None, :], 0), axis=1)
    rows_in, cols_in = ordered // 128, ordered % 128
    parity = rows_in % 2
    pair = rows_in // 2
    before = jnp.concatenate([jnp.full((1,), -1, jnp.int32), pair[:-1]])
    pairs = jnp.arange(64, dtype=jnp.int32)
    same = pair[None, :] == pairs[:, None]
    upto = jnp.sum((pair[None, :] <= pairs[:, None]).astype(jnp.int32), axis=1)
    ints = jnp.concatenate([(cols_in // 2) * 2 + (cols_in + parity) % 2, jnp.maximum(upto - 1, 0)])
    floats = jnp.concatenate(
        [(pair == before).astype(jnp.float32), parity.astype(jnp.float32), jnp.any(same, axis=1).astype(jnp.float32)]
    )
    return rank[None, :], ints, floats


def body(source, blocks, row_index, col_index, live_count):
    rank, ints, floats = tables(row_index, col_index, live_count)
    f32, bf16 = jnp.float32, jnp.bfloat16
    vmem = pltpu.VMEM
    dma = pltpu.SemaphoreType.DMA
    n = ITERS * GROUPS
    return pl.pallas_call(
        kernel,
        out_shape=jax.ShapeDtypeStruct(source.shape, f32),
        in_specs=[
            pl.BlockSpec(memory_space=pl.ANY),
            pl.BlockSpec(memory_space=pl.ANY),
            pl.BlockSpec(memory_space=vmem),
            pl.BlockSpec(memory_space=pltpu.SMEM),
            pl.BlockSpec(memory_space=pltpu.SMEM),
        ],
        out_specs=pl.BlockSpec(memory_space=vmem),
        scratch_shapes=[
            vmem((ITERS * 128, 64, 128), f32),
            vmem((128, 128, 128), bf16),
            vmem((128, 128, 128), bf16),
            vmem((SLOTS, 128, 128), bf16),
            vmem((SLOTS // 2 * 128, 128), f32),
            vmem((SLOTS, 64, 128), f32),
            vmem((64, 64, SLOTS), f32),
            vmem((SLOTS, SLOTS), bf16),
            vmem((GROUPS * ZN * TILES, 64, 128), f32),
            vmem((GROUPS * ZN * TILES, 64, 128), f32),
            vmem((n * ZN * TILES, 64, 128), f32),
            vmem((n * 2 * SPAN, 64, 128), f32),
            vmem((n * 2 * SPAN, 64, 128), f32),
            vmem((GROUPS * TILES, 64, 128), f32),
            vmem((8, 64, 128), f32),
            dma((n * 20,)),
            dma((n * 20,)),
            dma((n * ZN,)),
            dma((n * ZN,)),
            dma((n * 8,)),
            dma((n * 8,)),
            dma((4,)),
            dma,
        ],
        compiler_params=pltpu.CompilerParams(collective_id=0, has_side_effects=True, vmem_limit_bytes=62 << 20),
        name="bounces",
    )(source, jnp.transpose(blocks, (1, 2, 0)), rank, ints, floats)


def solution(mesh):
    specs = (P(("row", "col"), None, None),) * 2 + (P(("row", "col")),) * 3
    return jax.shard_map(body, mesh=mesh, in_specs=specs, out_specs=specs[0], check_vma=False)
```

```python
import jax
import jax.numpy as jnp
from jax import lax
from jax.experimental import pallas as pl
from jax.experimental.pallas import tpu as pltpu
from jax.sharding import PartitionSpec as P

MESH = pl.DeviceIdType.MESH
ITERS = 2
GROUPS = 2
TILES = 4
SLOTS = 256
ROWS = 16
ZN = 8
ZSHIFT = (4, 3, 5, 2, 6, 1, 7, 0)
PIECES = 8
LINES = (0, 3, 1, 2)
SPAN = 14


def rem(a, n):
    return lax.rem(a, n)


ORDER = (
    16, 0, 1, 2, 3, 4, 5, 6, 17, 18, 7, 23, 24, 8, 19, 20, 9, 25, 26, 10, 11, 12, 21, 30, 13, 22, 27, 14, 32, 33, 15,
    39, 40, 28, 29, 31, 34, 35, 38, 36, 37, 72, 41, 44, 42, 43, 45, 46, 47, 73, 74, 48, 79, 80, 49, 75, 76, 50, 81,
    82, 51, 52, 77, 86, 53, 78, 83, 54, 55, 56, 88, 89, 95, 96, 84, 85, 87, 57, 58, 90, 59, 60, 91, 94, 92, 93, 97,
    100, 98, 99, 61, 101, 62, 102, 63, 103, 64, 104, 105, 65, 106, 66, 107, 67, 108, 68, 109, 110, 111, 112, 69, 70,
    113, 114, 115, 116, 71, 117, 118, 119, 120, 128, 129, 121, 134, 135, 122, 130, 131, 123, 136, 137, 124, 132, 141,
    125, 133, 138, 126, 143, 144, 150, 151, 139, 140, 142, 145, 146, 149, 127, 147, 148, 152, 155, 153, 154, 156, 184,
    183, 190, 189, 186, 185, 192, 191, 157, 158, 188, 199, 159, 187, 198, 160, 193, 196, 161, 205, 206, 162, 197, 200,
    163, 194, 195, 164, 202, 203, 201, 165, 166, 167, 204, 207, 210, 209, 168, 169, 208, 170, 171, 212, 211, 213, 214,
    215, 216, 172, 217, 173, 218, 174, 219, 175, 220, 221, 222, 176, 177, 223, 224, 178, 225, 226, 179, 180, 181, 227,
    228, 229, 230, 182, 231, 232, 233, 234, 235, 236, 237,
)


def kernel(
    src_hbm, blk_hbm, mi, mf, out_ref,
    xg, xs0, xs1, a_ref, wide, c_ref, raw, po, px, cx, rp, sp, fx, srcv,
    ag_s, ag_r, cx_s, cx_r, rs_s, rs_r, blk_sem, src_sem,
):
    xs = (xs0, xs1)
    row, col = lax.axis_index("row"), lax.axis_index("col")
    y, x = row // 4, rem(row, 4)
    z, h = col // 2, rem(col, 2)

    def at(i, j):
        return rem(y + i * h + j * (1 - h), 4) * 4 + rem(x + i * (1 - h) + j * h, 4)

    def zcol(d):
        return rem(z + d, ZN) * 2 + h

    partner = z * 2 + (1 - h)

    blk_copies = [
        pltpu.make_async_copy(blk_hbm.at[:, pl.ds(8 * n, 8)], raw.at[:, pl.ds(8 * n, 8)], blk_sem.at[n]) for n in range(4)
    ]
    src_copy = pltpu.make_async_copy(src_hbm, srcv, src_sem)
    src_copy.start()
    for copy in blk_copies:
        copy.start()

    barrier = pltpu.get_barrier_semaphore()
    peers = [(at(1, 0), col), (at(3, 0), col), (at(0, 1), col), (at(0, 3), col)]
    peers += [(row, zcol(1)), (row, zcol(7)), (row, partner)]
    for peer in peers:
        pl.semaphore_signal(barrier, inc=1, device_id=peer, device_id_type=MESH)

    lane = lax.broadcasted_iota(jnp.int32, (64, 128), 1)
    low = lane < 64
    half = jnp.where(lax.broadcasted_iota(jnp.int32, (8, 128), 1) < 64, 1.0, 0.0).astype(jnp.float32)
    flip = 1.0 - 2.0 * half

    src_copy.wait()
    for j in range(TILES):
        even, odd = srcv[2 * j], srcv[2 * j + 1]
        xg[row * 8 + j] = jnp.where(low, even, pltpu.roll(odd, 64, 1))
        xg[row * 8 + TILES + j] = jnp.where(low, pltpu.roll(even, 64, 1), odd)

    pl.semaphore_wait(barrier, len(peers))


    def tile0(b, g, r):
        return b * 128 + r * 8 + g * TILES

    def ag(b, g, k, r, part, dest):
        ref = xg.at[pl.ds(tile0(b, g, r) + 2 * part, 2)]
        i = (b * GROUPS + g) * 30 + k
        return pltpu.make_async_remote_copy(
            src_ref=ref, dst_ref=ref, send_sem=ag_s.at[i], recv_sem=ag_r.at[i], device_id=(dest, col), device_id_type=MESH
        )

    pending = []

    def go(copy):
        copy.start()
        pending.append(copy)

    def split(b, g, r, t0=0, n=TILES):
        for t in range(t0, t0 + n):
            tile = xg[tile0(b, g, r) + t]
            for v, val in enumerate((tile, pltpu.roll(tile, 64, 1))):
                hi = val.astype(jnp.bfloat16)
                lo = (val - hi.astype(jnp.float32)).astype(jnp.bfloat16)
                at_ = (r * TILES + t) * 2 + v
                xs[g][at_, pl.ds(0, 64), :] = hi
                xs[g][at_, pl.ds(64, 64), :] = lo

    ahead, back = (at(1, 0), at(3, 0)), (at(0, 1), at(0, 3))

    def both_ways(b, g, k, r, part, ring):
        near, far = (ring[0], ring[1]) if part == 0 else (ring[1], ring[0])
        go(ag(b, g, k + part, r, part, near))
        go(ag(b, g, k + 3 - part, r, part, far))

    def gather_own(b, g):
        for k, ring in ((0, ahead), (6, back)):
            go(ag(b, g, k, row, 0, ring[0]))
            go(ag(b, g, k + 1, row, 1, ring[1]))
        for k, ring in ((0, ahead), (6, back)):
            go(ag(b, g, k + 2, row, 1, ring[0]))
            go(ag(b, g, k + 3, row, 0, ring[1]))

    def first(b, g, k):
        r = (at(3, 0), at(1, 0), at(3, 0), at(1, 0), at(2, 0), at(2, 0))[k]
        part = (0, 1, 1, 0, 0, 1)[k]
        ag(b, g, k, r, part, row).wait_recv()
        if k < 2:
            go(ag(b, g, 4 + k, r, part, ahead[k]))
        both_ways(b, g, 6 + 6 * (1, 2, 1, 2, 3, 3)[k], r, part, back)
        split(b, g, r, 2 * part, 2)

    def second(b, g, li, k):
        r = at(LINES[li], (3, 1, 3, 1, 2, 2)[k])
        part = (0, 1, 1, 0, 0, 1)[k]
        ag(b, g, 6 + 6 * li + k, r, part, row).wait_recv()
        if k < 2:
            go(ag(b, g, 10 + 6 * li + k, r, part, back[k]))
        split(b, g, r, 2 * part, 2)


    def turn_blocks(n):
        if n % 2 == 0:
            blk_copies[n // 2].wait()
        for i in range(4 * n, 4 * n + 4):
            pair = jnp.concatenate([raw[0, i], raw[1, i]], axis=0)
            wide[pl.ds(i, SLOTS, stride=32), :] = jnp.transpose(pair, (1, 0))

    def pack_blocks(n):
        def one(it, carry):
            for u in range(4):
                s = it * 4 + u
                val = wide[pl.ds(pl.multiple_of(s * 32, 32), 32), :]
                turned = pltpu.roll(val, 64, 1)
                low32 = low[:32]
                both = jnp.concatenate([jnp.where(low32, val, turned), jnp.where(low32, turned, val)], axis=0)
                hi = both.astype(jnp.bfloat16)
                a_ref[s, pl.ds(0, 64), :] = hi
                a_ref[s, pl.ds(64, 64), :] = (both - hi.astype(jnp.float32)).astype(jnp.bfloat16)
            return carry

        lax.fori_loop(8 * n, 8 * n + 8, one, 0)


    def products(g, piece):
        start = piece * (SLOTS // PIECES)

        acc = c_ref[start - 1] if piece else jnp.zeros((64, 128), jnp.float32)
        slots = range(start, start + SLOTS // PIECES)
        found = [jnp.dot(a_ref[mi[SLOTS + 64 + p]], xs[g][mi[p]], preferred_element_type=jnp.float32) for p in slots]
        for p, both in zip(slots, found):
            mask = half + mf[SLOTS + p] * flip
            both = ((both[:64] + both[64:]).reshape(8, 8, 128) * mask[None]).reshape(64, 128)
            acc = acc * mf[p] + both
            c_ref[p] = acc

    def partial_sum(zc, core, t):
        q = (zc * 2 + core) * TILES + t
        return c_ref[mi[SLOTS + q]] * mf[2 * SLOTS + q]

    def cx_copy(b, g, o):
        i = (b * GROUPS + g) * ZN + o
        return pltpu.make_async_remote_copy(
            src_ref=px.at[pl.ds((g * ZN + o) * TILES, TILES)], dst_ref=cx.at[pl.ds(i * TILES, TILES)],
            send_sem=cx_s.at[i], recv_sem=cx_r.at[i], device_id=(row, partner), device_id_type=MESH,
        )

    def sums_out(b, g):
        if b:
            for o in range(ZN):
                cx_copy(b - 1, g, o).wait_send()
        for o in range(ZN):
            for t in range(TILES):
                px[(g * ZN + o) * TILES + t] = partial_sum(rem(z + ZSHIFT[o], ZN), 1 - h, t)
            if o:
                cx_copy(b, g, o - 1).start()

    def sums_own(b, g):
        for o in range(ZN):
            for t in range(TILES):
                po[(g * ZN + o) * TILES + t] = partial_sum(rem(z + ZSHIFT[o], ZN), h, t)
            if o == 0:
                cx_copy(b, g, ZN - 1).start()


    def rs_copy(b, g, side, m):
        i = (b * GROUPS + g) * 2 + side
        at_ = pl.ds(i * SPAN + m, 1)
        return pltpu.make_async_remote_copy(
            src_ref=sp.at[at_], dst_ref=rp.at[at_], send_sem=rs_s.at[i * SPAN + m], recv_sem=rs_r.at[i * SPAN + m],
            device_id=(row, zcol(1 if side == 0 else 7)), device_id_type=MESH,
        )

    def chip_sum(b, g, o, t):
        return po[(g * ZN + o) * TILES + t] + cx[((b * GROUPS + g) * ZN + o) * TILES + t]

    def reduce_step(b, g, m):
        q, n = m // 2, m % 2
        t, chain = (q + 1) // 2, q % 2
        if n == 0:
            for o in (2 * t - 1, 2 * t) if chain else (0,) if t == 0 else ():
                cx_copy(b, g, o).wait_recv()
        for side in (0, 1):
            base = ((b * GROUPS + g) * 2 + side) * SPAN
            o = 0 if t == 0 else 2 * t - 1 + side
            val = chip_sum(b, g, o, 2 * ((side + chain) % 2) + n)
            if q > 1:
                rs_copy(b, g, side, m - 4).wait_recv()
                val = val + rp[base + m - 4]
            sp[base + m] = val
        for side in (0, 1):
            go(rs_copy(b, g, side, m))

    def reduce_last(b, g):
        cx_copy(b, g, ZN - 1).wait_recv()
        for side in (0, 1):
            for m in range(10, 14):
                rs_copy(b, g, side, m).wait_recv()
        base = (b * GROUPS + g) * 2 * SPAN
        for n in range(TILES):
            val = xg[tile0(0, g, row) + n] + chip_sum(b, g, ZN - 1, n)
            for side in (0, 1):
                m = 12 if n // 2 == side else 10
                val = val + rp[base + side * SPAN + m + n % 2]
            if b + 1 < ITERS:
                xg[tile0(b + 1, g, row) + n] = val
            else:
                fx[g * TILES + n] = val
        if b + 1 < ITERS:
            gather_own(b + 1, g)
            split(b + 1, g, row)

    tasks = []
    for n in range(8):
        tasks.append(lambda n=n: turn_blocks(n))
    for n in range(8):
        tasks.append(lambda n=n: pack_blocks(n))
    for b in range(ITERS):
        for g in range(GROUPS):
            if b == 0:
                tasks.append(lambda b=b, g=g: (gather_own(b, g), split(b, g, row)))
            for k in range(6):
                tasks.append(lambda b=b, g=g, k=k: first(b, g, k))
            for li in range(4):
                for k in range(4):
                    tasks.append(lambda b=b, g=g, li=li, k=k: second(b, g, li, k))
            for li in range(4):
                for k in range(4, 6):
                    tasks.append(lambda b=b, g=g, li=li, k=k: second(b, g, li, k))
            for piece in range(PIECES):
                tasks.append(lambda g=g, piece=piece: products(g, piece))
            tasks.append(lambda b=b, g=g: sums_out(b, g))
            tasks.append(lambda b=b, g=g: sums_own(b, g))
            for m in range(14):
                tasks.append(lambda b=b, g=g, m=m: reduce_step(b, g, m))
            tasks.append(lambda b=b, g=g: reduce_last(b, g))
    for n in ORDER:
        tasks[n]()

    for j in range(TILES):
        first, second = fx[j], fx[TILES + j]
        out_ref[2 * j] = jnp.where(low, first, pltpu.roll(second, 64, 1))
        out_ref[2 * j + 1] = jnp.where(low, pltpu.roll(first, 64, 1), second)

    for copy in pending:
        copy.wait_send()
    for g in range(GROUPS):
        for o in range(ZN):
            cx_copy(ITERS - 1, g, o).wait_send()


def tables(row_index, col_index, live_count):
    slots = jnp.arange(SLOTS, dtype=jnp.int32)
    rows = jnp.where(slots < live_count[0], row_index, 128)
    key = rows * SLOTS + slots
    rank = jnp.sum((key[None, :] < key[:, None]).astype(jnp.int32), axis=1)
    packed = key * 128 + col_index
    ordered = jnp.sum(jnp.where(rank[None, :] == slots[:, None], packed[None, :], 0), axis=1)
    keys_in, cols_in = ordered // 128, ordered % 128
    rows_in, slots_in = keys_in // SLOTS, keys_in % SLOTS
    parity = rows_in % 2
    pair = rows_in // 2
    before = jnp.concatenate([jnp.full((1,), -1, jnp.int32), pair[:-1]])
    pairs = jnp.arange(64, dtype=jnp.int32)
    same = pair[None, :] == pairs[:, None]
    upto = jnp.sum((pair[None, :] <= pairs[:, None]).astype(jnp.int32), axis=1)
    ints = jnp.concatenate([(cols_in // 2) * 2 + (cols_in + parity) % 2, jnp.maximum(upto - 1, 0), slots_in])
    floats = jnp.concatenate(
        [(pair == before).astype(jnp.float32), parity.astype(jnp.float32), jnp.any(same, axis=1).astype(jnp.float32)]
    )
    return ints, floats


def body(source, blocks, row_index, col_index, live_count):
    ints, floats = tables(row_index, col_index, live_count)
    f32, bf16 = jnp.float32, jnp.bfloat16
    vmem = pltpu.VMEM
    dma = pltpu.SemaphoreType.DMA
    n = ITERS * GROUPS
    return pl.pallas_call(
        kernel,
        out_shape=jax.ShapeDtypeStruct(source.shape, f32),
        in_specs=[
            pl.BlockSpec(memory_space=pl.ANY),
            pl.BlockSpec(memory_space=pl.ANY),
            pl.BlockSpec(memory_space=pltpu.SMEM),
            pl.BlockSpec(memory_space=pltpu.SMEM),
        ],
        out_specs=pl.BlockSpec(memory_space=vmem),
        scratch_shapes=[
            vmem((ITERS * 128, 64, 128), f32),
            vmem((128, 128, 128), bf16),
            vmem((128, 128, 128), bf16),
            vmem((SLOTS, 128, 128), bf16),
            vmem((SLOTS * 32, 128), f32),
            vmem((SLOTS, 64, 128), f32),
            vmem((2, 32, 64, SLOTS), f32),
            vmem((GROUPS * ZN * TILES, 64, 128), f32),
            vmem((GROUPS * ZN * TILES, 64, 128), f32),
            vmem((n * ZN * TILES, 64, 128), f32),
            vmem((n * 2 * SPAN, 64, 128), f32),
            vmem((n * 2 * SPAN, 64, 128), f32),
            vmem((GROUPS * TILES, 64, 128), f32),
            vmem((8, 64, 128), f32),
            dma((n * 30,)),
            dma((n * 30,)),
            dma((n * ZN,)),
            dma((n * ZN,)),
            dma((n * 2 * SPAN,)),
            dma((n * 2 * SPAN,)),
            dma((4,)),
            dma,
        ],
        compiler_params=pltpu.CompilerParams(collective_id=0, has_side_effects=True, vmem_limit_bytes=62 << 20),
        name="bounces",
    )(source, jnp.transpose(blocks, (1, 2, 0)).reshape(2, 32, 64, SLOTS), ints, floats)


def solution(mesh):
    specs = (P(("row", "col"), None, None),) * 2 + (P(("row", "col")),) * 3
    return jax.shard_map(body, mesh=mesh, in_specs=specs, out_specs=specs[0], check_vma=False)
```

```python
import jax
import jax.numpy as jnp
from jax import lax
from jax.experimental import pallas as pl
from jax.experimental.pallas import tpu as pltpu
from jax.sharding import PartitionSpec as P

MESH = pl.DeviceIdType.MESH
ITERS = 2
GROUPS = 2
TILES = 4
SLOTS = 256
ROWS = 16
ZN = 8
ZSHIFT = (4, 3, 5, 2, 6, 1, 7, 0)
PIECES = 8
LINES = (0, 3, 1, 2)
SPAN = 14


def rem(a, n):
    return lax.rem(a, n)


ORDER = (
    16, 0, 1, 2, 3, 4, 5, 17, 18, 6, 23, 24, 7, 19, 20, 8, 9, 25, 26, 10, 21, 30, 11, 22, 27, 12, 32, 33, 13, 14, 39,
    40, 15, 28, 29, 31, 34, 35, 38, 36, 72, 37, 41, 44, 42, 43, 45, 46, 47, 48, 49, 73, 74, 50, 51, 79, 80, 52, 53,
    54, 55, 56, 75, 76, 81, 82, 57, 58, 77, 86, 59, 60, 83, 78, 89, 88, 61, 95, 96, 62, 85, 84, 63, 87, 90, 64, 91,
    94, 65, 97, 92, 66, 93, 100, 67, 99, 98, 68, 101, 102, 103, 104, 69, 105, 106, 107, 70, 108, 109, 110, 111, 112,
    113, 114, 115, 116, 71, 128, 117, 118, 129, 130, 119, 135, 136, 120, 131, 132, 121, 137, 138, 122, 133, 142, 123,
    134, 139, 124, 144, 145, 125, 151, 152, 126, 140, 141, 143, 146, 147, 150, 148, 149, 127, 184, 153, 156, 154, 155,
    157, 158, 159, 160, 161, 185, 186, 162, 163, 191, 192, 164, 165, 166, 167, 168, 187, 188, 193, 194, 169, 170, 189,
    198, 171, 172, 195, 190, 201, 200, 173, 207, 208, 174, 197, 196, 175, 199, 202, 176, 203, 206, 177, 209, 204, 178,
    205, 212, 179, 211, 210, 180, 213, 214, 215, 216, 181, 217, 218, 219, 182, 220, 221, 222, 223, 224, 225, 226, 227,
    228, 183, 229, 230, 231, 232, 233, 234, 235, 236, 237, 238, 239,
)


def kernel(
    src_hbm, blk_hbm, mi, mf, out_ref,
    xg, xs0, xs1, a_ref, wide, c_ref, raw, po, px, cx, rp, sp, fx, srcv,
    ag_s, ag_r, cx_s, cx_r, rs_s, rs_r, blk_sem, src_sem,
):
    xs = (xs0, xs1)
    row, col = lax.axis_index("row"), lax.axis_index("col")
    y, x = row // 4, rem(row, 4)
    z, h = col // 2, rem(col, 2)

    def at(i, j):
        return rem(y + i * h + j * (1 - h), 4) * 4 + rem(x + i * (1 - h) + j * h, 4)

    def zcol(d):
        return rem(z + d, ZN) * 2 + h

    partner = z * 2 + (1 - h)

    blk_copies = [
        pltpu.make_async_copy(blk_hbm.at[:, pl.ds(8 * n, 8)], raw.at[:, pl.ds(8 * n, 8)], blk_sem.at[n]) for n in range(4)
    ]
    src_copy = pltpu.make_async_copy(src_hbm, srcv, src_sem)
    src_copy.start()
    for copy in blk_copies:
        copy.start()

    barrier = pltpu.get_barrier_semaphore()
    peers = [(at(1, 0), col), (at(3, 0), col), (at(0, 1), col), (at(0, 3), col)]
    peers += [(row, zcol(1)), (row, zcol(7)), (row, partner)]
    for peer in peers:
        pl.semaphore_signal(barrier, inc=1, device_id=peer, device_id_type=MESH)

    lane = lax.broadcasted_iota(jnp.int32, (64, 128), 1)
    low = lane < 64
    half = jnp.where(lax.broadcasted_iota(jnp.int32, (8, 128), 1) < 64, 1.0, 0.0).astype(jnp.float32)
    flip = 1.0 - 2.0 * half

    src_copy.wait()
    for j in range(TILES):
        even, odd = srcv[2 * j], srcv[2 * j + 1]
        xg[row * 8 + j] = jnp.where(low, even, pltpu.roll(odd, 64, 1))
        xg[row * 8 + TILES + j] = jnp.where(low, pltpu.roll(even, 64, 1), odd)

    pl.semaphore_wait(barrier, len(peers))


    def tile0(b, g, r):
        return b * 128 + r * 8 + g * TILES

    def ag(b, g, k, r, part, dest):
        ref = xg.at[pl.ds(tile0(b, g, r) + 2 * part, 2)]
        i = (b * GROUPS + g) * 30 + k
        return pltpu.make_async_remote_copy(
            src_ref=ref, dst_ref=ref, send_sem=ag_s.at[i], recv_sem=ag_r.at[i], device_id=(dest, col), device_id_type=MESH
        )

    pending = []

    def go(copy):
        copy.start()
        pending.append(copy)

    def split(b, g, r, t0=0, n=TILES):
        for t in range(t0, t0 + n):
            tile = xg[tile0(b, g, r) + t]
            for v, val in enumerate((tile, pltpu.roll(tile, 64, 1))):
                hi = val.astype(jnp.bfloat16)
                lo = (val - hi.astype(jnp.float32)).astype(jnp.bfloat16)
                at_ = (r * TILES + t) * 2 + v
                xs[g][at_, pl.ds(0, 64), :] = hi
                xs[g][at_, pl.ds(64, 64), :] = lo

    ahead, back = (at(1, 0), at(3, 0)), (at(0, 1), at(0, 3))

    def both_ways(b, g, k, r, part, ring):
        near, far = (ring[0], ring[1]) if part == 0 else (ring[1], ring[0])
        go(ag(b, g, k + part, r, part, near))
        go(ag(b, g, k + 3 - part, r, part, far))

    def gather_own(b, g):
        for k, ring in ((0, ahead), (6, back)):
            go(ag(b, g, k, row, 0, ring[0]))
            go(ag(b, g, k + 1, row, 1, ring[1]))
        for k, ring in ((0, ahead), (6, back)):
            go(ag(b, g, k + 2, row, 1, ring[0]))
            go(ag(b, g, k + 3, row, 0, ring[1]))

    def first(b, g, k):
        r = (at(3, 0), at(1, 0), at(3, 0), at(1, 0), at(2, 0), at(2, 0))[k]
        part = (0, 1, 1, 0, 0, 1)[k]
        ag(b, g, k, r, part, row).wait_recv()
        if k < 2:
            go(ag(b, g, 4 + k, r, part, ahead[k]))
        both_ways(b, g, 6 + 6 * (1, 2, 1, 2, 3, 3)[k], r, part, back)
        split(b, g, r, 2 * part, 2)

    def second(b, g, li, k):
        r = at(LINES[li], (3, 1, 3, 1, 2, 2)[k])
        part = (0, 1, 1, 0, 0, 1)[k]
        ag(b, g, 6 + 6 * li + k, r, part, row).wait_recv()
        if k < 2:
            go(ag(b, g, 10 + 6 * li + k, r, part, back[k]))
        split(b, g, r, 2 * part, 2)


    def turn_blocks(n):
        if n % 2 == 0:
            blk_copies[n // 2].wait()
        for i in range(4 * n, 4 * n + 4):
            pair = jnp.concatenate([raw[0, i], raw[1, i]], axis=0)
            wide[pl.ds(i, SLOTS, stride=32), :] = jnp.transpose(pair, (1, 0))

    def pack_blocks(n):
        def one(it, carry):
            for u in range(4):
                s = it * 4 + u
                val = wide[pl.ds(pl.multiple_of(s * 32, 32), 32), :]
                turned = pltpu.roll(val, 64, 1)
                low32 = low[:32]
                both = jnp.concatenate([jnp.where(low32, val, turned), jnp.where(low32, turned, val)], axis=0)
                hi = both.astype(jnp.bfloat16)
                a_ref[s, pl.ds(0, 64), :] = hi
                a_ref[s, pl.ds(64, 64), :] = (both - hi.astype(jnp.float32)).astype(jnp.bfloat16)
            return carry

        lax.fori_loop(8 * n, 8 * n + 8, one, 0)


    def products(g, piece):
        start = piece * (SLOTS // PIECES)

        acc = c_ref[start - 1] if piece else jnp.zeros((64, 128), jnp.float32)
        slots = range(start, start + SLOTS // PIECES)
        found = [jnp.dot(a_ref[mi[SLOTS + 64 + p]], xs[g][mi[p]], preferred_element_type=jnp.float32) for p in slots]
        for p, both in zip(slots, found):
            mask = half + mf[SLOTS + p] * flip
            both = ((both[:64] + both[64:]).reshape(8, 8, 128) * mask[None]).reshape(64, 128)
            acc = acc * mf[p] + both
            c_ref[p] = acc

    def partial_sum(zc, core, t):
        q = (zc * 2 + core) * TILES + t
        return c_ref[mi[SLOTS + q]] * mf[2 * SLOTS + q]

    def cx_copy(b, g, o):
        i = (b * GROUPS + g) * ZN + o
        return pltpu.make_async_remote_copy(
            src_ref=px.at[pl.ds((g * ZN + o) * TILES, TILES)], dst_ref=cx.at[pl.ds(i * TILES, TILES)],
            send_sem=cx_s.at[i], recv_sem=cx_r.at[i], device_id=(row, partner), device_id_type=MESH,
        )

    def sums_out(b, g):
        if b:
            for o in range(ZN):
                cx_copy(b - 1, g, o).wait_send()
        for o in range(ZN):
            for t in range(TILES):
                px[(g * ZN + o) * TILES + t] = partial_sum(rem(z + ZSHIFT[o], ZN), 1 - h, t)
            if o:
                cx_copy(b, g, o - 1).start()

    def sums_own(b, g):
        for o in range(ZN):
            for t in range(TILES):
                po[(g * ZN + o) * TILES + t] = partial_sum(rem(z + ZSHIFT[o], ZN), h, t)
            if o == 0:
                cx_copy(b, g, ZN - 1).start()


    def rs_copy(b, g, side, m):
        i = (b * GROUPS + g) * 2 + side
        at_ = pl.ds(i * SPAN + m, 1)
        return pltpu.make_async_remote_copy(
            src_ref=sp.at[at_], dst_ref=rp.at[at_], send_sem=rs_s.at[i * SPAN + m], recv_sem=rs_r.at[i * SPAN + m],
            device_id=(row, zcol(1 if side == 0 else 7)), device_id_type=MESH,
        )

    def chip_sum(b, g, o, t):
        return po[(g * ZN + o) * TILES + t] + cx[((b * GROUPS + g) * ZN + o) * TILES + t]

    def reduce_step(b, g, m):
        q, n = m // 2, m % 2
        t, chain = (q + 1) // 2, q % 2
        if n == 0:
            for o in (2 * t - 1, 2 * t) if chain else (0,) if t == 0 else ():
                cx_copy(b, g, o).wait_recv()
        for side in (0, 1):
            base = ((b * GROUPS + g) * 2 + side) * SPAN
            o = 0 if t == 0 else 2 * t - 1 + side
            val = chip_sum(b, g, o, 2 * ((side + chain) % 2) + n)
            if q > 1:
                rs_copy(b, g, side, m - 4).wait_recv()
                val = val + rp[base + m - 4]
            sp[base + m] = val
        for side in (0, 1):
            go(rs_copy(b, g, side, m))

    def reduce_last(b, g):
        cx_copy(b, g, ZN - 1).wait_recv()
        for side in (0, 1):
            for m in range(10, 14):
                rs_copy(b, g, side, m).wait_recv()
        base = (b * GROUPS + g) * 2 * SPAN
        for n in range(TILES):
            val = xg[tile0(0, g, row) + n] + chip_sum(b, g, ZN - 1, n)
            for side in (0, 1):
                m = 12 if n // 2 == side else 10
                val = val + rp[base + side * SPAN + m + n % 2]
            if b + 1 < ITERS:
                xg[tile0(b + 1, g, row) + n] = val
            else:
                fx[g * TILES + n] = val
    tasks = []
    for n in range(8):
        tasks.append(lambda n=n: turn_blocks(n))
    for n in range(8):
        tasks.append(lambda n=n: pack_blocks(n))
    for b in range(ITERS):
        for g in range(GROUPS):
            tasks.append(lambda b=b, g=g: (gather_own(b, g), split(b, g, row)))
            for k in range(6):
                tasks.append(lambda b=b, g=g, k=k: first(b, g, k))
            for li in range(4):
                for k in range(4):
                    tasks.append(lambda b=b, g=g, li=li, k=k: second(b, g, li, k))
            for li in range(4):
                for k in range(4, 6):
                    tasks.append(lambda b=b, g=g, li=li, k=k: second(b, g, li, k))
            for piece in range(PIECES):
                tasks.append(lambda g=g, piece=piece: products(g, piece))
            tasks.append(lambda b=b, g=g: sums_out(b, g))
            tasks.append(lambda b=b, g=g: sums_own(b, g))
            for m in range(14):
                tasks.append(lambda b=b, g=g, m=m: reduce_step(b, g, m))
            tasks.append(lambda b=b, g=g: reduce_last(b, g))
    for n in ORDER:
        tasks[n]()

    for j in range(TILES):
        first, second = fx[j], fx[TILES + j]
        out_ref[2 * j] = jnp.where(low, first, pltpu.roll(second, 64, 1))
        out_ref[2 * j + 1] = jnp.where(low, pltpu.roll(first, 64, 1), second)

    for copy in pending:
        copy.wait_send()
    for g in range(GROUPS):
        for o in range(ZN):
            cx_copy(ITERS - 1, g, o).wait_send()


def tables(row_index, col_index, live_count):
    slots = jnp.arange(SLOTS, dtype=jnp.int32)
    rows = jnp.where(slots < live_count[0], row_index, 128)
    key = rows * SLOTS + slots
    rank = jnp.sum((key[None, :] < key[:, None]).astype(jnp.int32), axis=1)
    packed = key * 128 + col_index
    ordered = jnp.sum(jnp.where(rank[None, :] == slots[:, None], packed[None, :], 0), axis=1)
    keys_in, cols_in = ordered // 128, ordered % 128
    rows_in, slots_in = keys_in // SLOTS, keys_in % SLOTS
    parity = rows_in % 2
    pair = rows_in // 2
    before = jnp.concatenate([jnp.full((1,), -1, jnp.int32), pair[:-1]])
    pairs = jnp.arange(64, dtype=jnp.int32)
    same = pair[None, :] == pairs[:, None]
    upto = jnp.sum((pair[None, :] <= pairs[:, None]).astype(jnp.int32), axis=1)
    ints = jnp.concatenate([(cols_in // 2) * 2 + (cols_in + parity) % 2, jnp.maximum(upto - 1, 0), slots_in])
    floats = jnp.concatenate(
        [(pair == before).astype(jnp.float32), parity.astype(jnp.float32), jnp.any(same, axis=1).astype(jnp.float32)]
    )
    return ints, floats


def body(source, blocks, row_index, col_index, live_count):
    ints, floats = tables(row_index, col_index, live_count)
    f32, bf16 = jnp.float32, jnp.bfloat16
    vmem = pltpu.VMEM
    dma = pltpu.SemaphoreType.DMA
    n = ITERS * GROUPS
    return pl.pallas_call(
        kernel,
        out_shape=jax.ShapeDtypeStruct(source.shape, f32),
        in_specs=[
            pl.BlockSpec(memory_space=pl.ANY),
            pl.BlockSpec(memory_space=pl.ANY),
            pl.BlockSpec(memory_space=pltpu.SMEM),
            pl.BlockSpec(memory_space=pltpu.SMEM),
        ],
        out_specs=pl.BlockSpec(memory_space=vmem),
        scratch_shapes=[
            vmem((ITERS * 128, 64, 128), f32),
            vmem((128, 128, 128), bf16),
            vmem((128, 128, 128), bf16),
            vmem((SLOTS, 128, 128), bf16),
            vmem((SLOTS * 32, 128), f32),
            vmem((SLOTS, 64, 128), f32),
            vmem((2, 32, 64, SLOTS), f32),
            vmem((GROUPS * ZN * TILES, 64, 128), f32),
            vmem((GROUPS * ZN * TILES, 64, 128), f32),
            vmem((n * ZN * TILES, 64, 128), f32),
            vmem((n * 2 * SPAN, 64, 128), f32),
            vmem((n * 2 * SPAN, 64, 128), f32),
            vmem((GROUPS * TILES, 64, 128), f32),
            vmem((8, 64, 128), f32),
            dma((n * 30,)),
            dma((n * 30,)),
            dma((n * ZN,)),
            dma((n * ZN,)),
            dma((n * 2 * SPAN,)),
            dma((n * 2 * SPAN,)),
            dma((4,)),
            dma,
        ],
        compiler_params=pltpu.CompilerParams(collective_id=0, has_side_effects=True, vmem_limit_bytes=62 << 20),
        name="bounces",
    )(source, jnp.transpose(blocks, (1, 2, 0)).reshape(2, 32, 64, SLOTS), ints, floats)


def solution(mesh):
    specs = (P(("row", "col"), None, None),) * 2 + (P(("row", "col")),) * 3
    return jax.shard_map(body, mesh=mesh, in_specs=specs, out_specs=specs[0], check_vma=False)
```
